128 devices in a mesh: ga: 8 (over y_hi, z), ka: 16 (over y_lo, x, core).
Axes of the slice: x: 4, y: 4 (y_hi: 2, y_lo: 2; y = y_hi * 2 + y_lo), z: 4, core: 2. Of those that a mesh axis runs over, the one named last changes fastest.
Arguments:
- amplitudes: float32 [14400, 2048], P(None, ('ka', 'ga')), may hold values from -6 to 6
- integrals: float32 [2048, 15360], P('ga', 'ka'), may hold values from -0.125 to 0.125
Outputs:
- residual: float32 [14400, 15360], P('ga', 'ka')
The draws below stay inside these ranges and needn't reach their ends.
All inputs are finite; a program needn't handle non-finite values.
Results may differ from the reference program's by a relative error of at most 0.00007.
Values sent between devices are 32-bit elements; how exact they have to be, the bound alone decides.
A program may use at most 128 MiB of HBM per device.

```python
import jax
import jax.numpy as jnp
from jax import lax

CD = 2048
IJ = 14400
AB = 15360


def level_of(own_key, shape, pieces, low, top_value):
    level = 1.0
    for position, blocks in pieces:
        heights = jax.random.uniform(jax.random.fold_in(jax.random.fold_in(own_key, 6), position), (blocks,), jnp.float32, low / len(pieces), top_value / len(pieces))
        level = level * jnp.repeat(jnp.exp(heights), shape[position] // blocks).reshape((-1,) + (1,) * (len(shape) - 1 - position))
    return level


def centred(own_key, extent, spread, reach, split=(), held_as=jnp.bfloat16):
    array = spread * jax.random.normal(own_key, extent, jnp.float32)
    if split:
        array = array * level_of(own_key, extent, split, -0.22, 0.18)
    return jnp.clip(array, -reach, reach).astype(held_as)


def setup_inputs(seed: int = 0) -> dict:
    key_list = jax.random.split(jax.random.key(seed), 3)
    amplitudes = centred(key_list[0], (IJ, CD), 1.0, 6.0, ((1, 128),), jnp.float32)
    integrals = centred(key_list[1], (CD, AB), CD ** -0.5, 0.125, ((0, 8), (1, 16)), jnp.float32)
    return {"amplitudes": amplitudes, "integrals": integrals}


def reference(amplitudes, integrals):
    ladder = jnp.dot(amplitudes, integrals, precision=lax.Precision.HIGHEST, preferred_element_type=jnp.float32)
    return 0.5 * ladder
```

```python
import jax
import jax.numpy as jnp
from jax import lax
from jax.sharding import PartitionSpec as P


def per_device(amplitudes, integrals):
    regrouped = lax.all_to_all(amplitudes, "ga", split_axis=0, concat_axis=1, tiled=True)
    full_rows = lax.all_gather(regrouped, "ka", axis=1, tiled=True)
    ladder = jnp.dot(
        full_rows,
        lax.all_gather(integrals, "ga", axis=0, tiled=True),
        precision=lax.Precision.HIGH,
        preferred_element_type=jnp.float32,
    )
    return 0.5 * ladder


def solution(mesh):
    placed = (P(None, ("ka", "ga")), P("ga", "ka"))
    return jax.shard_map(
        per_device, mesh=mesh, in_specs=placed, out_specs=P("ga", "ka"), check_vma=False
    )
```

```python
import functools

import jax
import jax.numpy as jnp
from jax import lax
from jax.experimental import pallas as pl
from jax.experimental.pallas import tpu as pltpu
from jax.sharding import PartitionSpec as P

MESH = pl.DeviceIdType.MESH


def _tile(n, cands):
    for c in cands:
        if n % c == 0:
            return c
    return n


def _split(x):
    hi = x.astype(jnp.bfloat16)
    lo = (x - hi.astype(jnp.float32)).astype(jnp.bfloat16)
    return hi, lo


def ladder_kernel(ng, nk, at_ref, bt_ref, ct_ref, a_full, b_full, ah, al, bh, bl,
                  sem_at, sem_a, sem_b, snd_at, snd_a, snd_b):
    g = lax.axis_index("ga")
    k = lax.axis_index("ka")
    cw = at_ref.shape[1]
    nb, bk = bt_ref.shape
    kb = ng * cw
    q = bk // kb
    rp = ct_ref.shape[1]

    barrier = pltpu.get_barrier_semaphore()
    for s in range(1, ng):
        pl.semaphore_signal(barrier, inc=1, device_id=(lax.rem(g + s, ng), k), device_id_type=MESH)
    for s in range(1, nk):
        pl.semaphore_signal(barrier, inc=1, device_id=(g, lax.rem(k + s, nk)), device_id_type=MESH)
    pl.semaphore_wait(barrier, ng - 1 + nk - 1)

    def a_rows(kk, gg):
        return a_full.at[pl.ds(pl.multiple_of(kk * kb + gg * cw, 8), cw), :]

    def a_block(kk):
        return a_full.at[pl.ds(pl.multiple_of(kk * kb, 8), kb), :]

    def b_cols(gg):
        return b_full.at[:, pl.ds(pl.multiple_of(gg * bk, 128), bk)]

    at_copies = []
    for s in range(1, ng):
        g2 = lax.rem(g + s, ng)
        c = pltpu.make_async_remote_copy(
            src_ref=at_ref.at[g2], dst_ref=a_rows(k, g), send_sem=snd_at.at[s],
            recv_sem=sem_at.at[g], device_id=(g2, k), device_id_type=MESH)
        c.start()
        at_copies.append(c)
    pltpu.make_async_copy(at_ref.at[g], a_rows(k, g), sem_at.at[g]).start()
    b_copies = []
    for s in range(1, ng):
        g2 = lax.rem(g + s, ng)
        c = pltpu.make_async_remote_copy(
            src_ref=bt_ref, dst_ref=b_cols(g), send_sem=snd_b.at[s],
            recv_sem=sem_b.at[g], device_id=(g2, k), device_id_type=MESH)
        c.start()
        b_copies.append(c)
    pltpu.make_async_copy(bt_ref, b_cols(g), sem_b.at[g]).start()

    ct_ref[...] = jnp.zeros_like(ct_ref)

    for s in range(ng):
        g2 = lax.rem(g + s, ng)
        pltpu.make_async_copy(at_ref.at[0], a_rows(k, g2), sem_at.at[g2]).wait()

    a_copies = []
    for s in range(1, nk):
        k2 = lax.rem(k + s, nk)
        c = pltpu.make_async_remote_copy(
            src_ref=a_block(k), dst_ref=a_block(k), send_sem=snd_a.at[s],
            recv_sem=sem_a.at[k], device_id=(g, k2), device_id_type=MESH)
        c.start()
        a_copies.append(c)

    tm = _tile(nb, (192, 240, 160, 128, 120, 96, 64, 48, 32, 16))
    tn = _tile(rp, (384, 640, 256, 128))
    nmt, nnt = nb // tm, rp // tn
    ra = _tile(bk, (32, 16, 8))
    rb = _tile(nb, (120, 96, 64, 48, 32, 16, 8))

    def chunk(i, carry):
        j = lax.rem(k // q + i, ng)
        pltpu.make_async_copy(bt_ref, b_cols(j), sem_b.at[j]).wait()
        for t in range(q):
            kk = j * q + t

            @pl.when(kk != k)
            def _():
                pltpu.make_async_copy(a_block(0), a_block(kk), sem_a.at[kk]).wait()

        k0 = pl.multiple_of(j * bk, 128)

        def split_a(r, c):
            r0 = pl.multiple_of(r * ra, 8)
            hi, lo = _split(a_full[pl.ds(k0 + r0, ra), :])
            ah[pl.ds(r0, ra), :] = hi
            al[pl.ds(r0, ra), :] = lo
            return c

        lax.fori_loop(0, bk // ra, split_a, 0)

        def split_b(r, c):
            r0 = pl.multiple_of(r * rb, 8)
            hi, lo = _split(b_full[pl.ds(r0, rb), pl.ds(k0, bk)])
            bh[pl.ds(r0, rb), :] = hi
            bl[pl.ds(r0, rb), :] = lo
            return c

        lax.fori_loop(0, nb // rb, split_b, 0)

        def mm(t, c):
            m0 = pl.multiple_of((t // nnt) * tm, 8)
            n0 = pl.multiple_of((t % nnt) * tn, 128)
            bh_t = bh[pl.ds(m0, tm), :]
            bl_t = bl[pl.ds(m0, tm), :]
            ah_t = ah[:, pl.ds(n0, tn)]
            al_t = al[:, pl.ds(n0, tn)]
            d = jnp.dot(bh_t, ah_t, preferred_element_type=jnp.float32)
            d = d + jnp.dot(bh_t, al_t, preferred_element_type=jnp.float32)
            d = d + jnp.dot(bl_t, ah_t, preferred_element_type=jnp.float32)
            ct_ref[pl.ds(m0, tm), pl.ds(n0, tn)] += d
            return c

        lax.fori_loop(0, nmt * nnt, mm, 0)
        return carry

    lax.fori_loop(0, ng, chunk, 0)

    for c in at_copies + b_copies + a_copies:
        c.wait_send()


def solution(mesh):
    ng = mesh.shape["ga"]
    nk = mesh.shape["ka"]

    def per_device(amplitudes, integrals):
        ij, cw = amplitudes.shape
        bk, nb = integrals.shape
        r = ij // ng
        rp = -(-r // 128) * 128
        cd = bk * ng
        at = amplitudes.reshape(ng, r, cw).transpose(0, 2, 1)
        at = jnp.pad(at, ((0, 0), (0, 0), (0, rp - r)))
        bt = integrals.T
        vmem = pltpu.VMEM
        ct = pl.pallas_call(
            functools.partial(ladder_kernel, ng, nk),
            out_shape=jax.ShapeDtypeStruct((nb, rp), jnp.float32),
            in_specs=[pl.BlockSpec(memory_space=vmem)] * 2,
            out_specs=pl.BlockSpec(memory_space=vmem),
            scratch_shapes=[
                vmem((cd, rp), jnp.float32),
                vmem((nb, cd), jnp.float32),
                vmem((bk, rp), jnp.bfloat16),
                vmem((bk, rp), jnp.bfloat16),
                vmem((nb, bk), jnp.bfloat16),
                vmem((nb, bk), jnp.bfloat16),
                pltpu.SemaphoreType.DMA((ng,)),
                pltpu.SemaphoreType.DMA((nk,)),
                pltpu.SemaphoreType.DMA((ng,)),
                pltpu.SemaphoreType.DMA((ng,)),
                pltpu.SemaphoreType.DMA((nk,)),
                pltpu.SemaphoreType.DMA((ng,)),
            ],
            compiler_params=pltpu.CompilerParams(
                collective_id=0, has_side_effects=True, vmem_limit_bytes=60 * 1024 * 1024
            ),
            cost_estimate=pl.CostEstimate(
                flops=6 * nb * rp * cd, bytes_accessed=4 * (cd * rp + nb * cd + nb * rp),
                transcendentals=0),
        )(at, bt)
        return (0.5 * ct[:, :r]).T

    placed = (P(None, ("ka", "ga")), P("ga", "ka"))
    return jax.shard_map(
        per_device, mesh=mesh, in_specs=placed, out_specs=P("ga", "ka"), check_vma=False
    )
```

```python
import jax
import jax.numpy as jnp
from jax import lax
from jax.sharding import PartitionSpec as P

CHUNKS = 5


def per_device(amplitudes, integrals):
    full_b = lax.all_gather(integrals, "ga", axis=0, tiled=True)
    regrouped = lax.all_to_all(amplitudes, "ga", split_axis=0, concat_axis=1, tiled=True)
    rows = regrouped.shape[0] // CHUNKS
    pieces = [regrouped[i * rows:(i + 1) * rows] for i in range(CHUNKS)]
    parts = []
    for i in range(CHUNKS):
        piece = pieces[i]
        if i >= 2:
            piece, _ = lax.optimization_barrier((piece, parts[i - 2]))
        full_rows = lax.all_gather(piece, "ka", axis=1, tiled=True)
        ladder = jnp.dot(
            full_rows,
            full_b,
            precision=lax.Precision.HIGH,
            preferred_element_type=jnp.float32,
        )
        parts.append(0.5 * ladder)
    return jnp.concatenate(parts, axis=0)


def solution(mesh):
    placed = (P(None, ("ka", "ga")), P("ga", "ka"))
    return jax.shard_map(
        per_device, mesh=mesh, in_specs=placed, out_specs=P("ga", "ka"), check_vma=False
    )
```

```python
import jax
import jax.numpy as jnp
from jax import lax
from jax.sharding import PartitionSpec as P


def per_device(ng, amplitudes, integrals):
    g = lax.axis_index("ga")
    received = [integrals]
    for s in range(1, ng):
        received.append(lax.ppermute(integrals, "ga", [(i, (i + s) % ng) for i in range(ng)]))
    by_shift = jnp.stack(received)
    full_b = jnp.take(by_shift, lax.rem(g - jnp.arange(ng) + ng, ng), axis=0)
    full_b = full_b.reshape(-1, integrals.shape[1])
    regrouped = lax.all_to_all(amplitudes, "ga", split_axis=0, concat_axis=1, tiled=True)
    full_rows = lax.all_gather(regrouped, "ka", axis=1, tiled=True)
    ladder = jnp.dot(
        full_rows,
        full_b,
        precision=lax.Precision.HIGH,
        preferred_element_type=jnp.float32,
    )
    return 0.5 * ladder


def solution(mesh):
    placed = (P(None, ("ka", "ga")), P("ga", "ka"))
    ng = mesh.shape["ga"]
    return jax.shard_map(
        lambda a, b: per_device(ng, a, b), mesh=mesh, in_specs=placed, out_specs=P("ga", "ka"),
        check_vma=False
    )
```

```python
import jax
import jax.numpy as jnp
from jax import lax
from jax.sharding import PartitionSpec as P


def per_device(ng, amplitudes, integrals):
    g = lax.axis_index("ga")
    bk, nb = integrals.shape
    bt = integrals.T
    full_bt = jnp.zeros((nb, bk * ng), jnp.float32)
    for s in range(ng):
        got = bt if s == 0 else lax.ppermute(bt, "ga", [(i, (i + s) % ng) for i in range(ng)])
        full_bt = lax.dynamic_update_slice(full_bt, got, (0, lax.rem(g - s + ng, ng) * bk))
    regrouped = lax.all_to_all(amplitudes, "ga", split_axis=0, concat_axis=1, tiled=True)
    full_rows = lax.all_gather(regrouped, "ka", axis=1, tiled=True)
    ladder = lax.dot_general(
        full_rows,
        full_bt,
        (((1,), (1,)), ((), ())),
        precision=lax.Precision.HIGH,
        preferred_element_type=jnp.float32,
    )
    return 0.5 * ladder


def solution(mesh):
    placed = (P(None, ("ka", "ga")), P("ga", "ka"))
    ng = mesh.shape["ga"]
    return jax.shard_map(
        lambda a, b: per_device(ng, a, b), mesh=mesh, in_specs=placed, out_specs=P("ga", "ka"),
        check_vma=False
    )
```

```python
import jax
import jax.numpy as jnp
from jax import lax
from jax.sharding import PartitionSpec as P


def per_device(ng, amplitudes, integrals):
    g = lax.axis_index("ga")
    bk, nb = integrals.shape
    nz = ng // 2
    yh, z = g // nz, lax.rem(g, nz)
    bt = integrals.T
    full_bt = lax.dynamic_update_slice(jnp.zeros((nb, bk * ng), jnp.float32), bt, (0, g * bk))
    offsets = [(1, dz) for dz in range(nz)] + [(0, dz) for dz in range(nz // 2, 0, -1)]
    offsets += [(0, dz) for dz in range(nz // 2 + 1, nz)]
    for dy, dz in offsets:
        pairs = [(i, ((i // nz + dy) % 2) * nz + (i % nz + dz) % nz) for i in range(ng)]
        got = lax.ppermute(bt, "ga", pairs)
        src = lax.rem(yh + dy, 2) * nz + lax.rem(z - dz + nz, nz)
        full_bt = lax.dynamic_update_slice(full_bt, got, (0, src * bk))
    regrouped = lax.all_to_all(amplitudes, "ga", split_axis=0, concat_axis=1, tiled=True)
    full_rows = lax.all_gather(regrouped, "ka", axis=1, tiled=True)
    ladder = lax.dot_general(
        full_rows,
        full_bt,
        (((1,), (1,)), ((), ())),
        precision=lax.Precision.HIGH,
        preferred_element_type=jnp.float32,
    )
    return 0.5 * ladder


def solution(mesh):
    placed = (P(None, ("ka", "ga")), P("ga", "ka"))
    ng = mesh.shape["ga"]
    return jax.shard_map(
        lambda a, b: per_device(ng, a, b), mesh=mesh, in_specs=placed, out_specs=P("ga", "ka"),
        check_vma=False
    )
```

```python
import jax
import jax.numpy as jnp
from jax import lax
from jax.sharding import PartitionSpec as P


def _offsets(ng):
    nz = ng // 2
    offsets = [(1, dz) for dz in range(nz)] + [(0, dz) for dz in range(nz // 2, 0, -1)]
    return nz, offsets + [(0, dz) for dz in range(nz // 2 + 1, nz)]


def per_device(ng, amplitudes, integrals):
    g = lax.axis_index("ga")
    bk, nb = integrals.shape
    nz, offsets = _offsets(ng)
    yh, z = g // nz, lax.rem(g, nz)
    pieces = amplitudes.reshape(ng, -1, amplitudes.shape[1])
    stack = lax.dynamic_update_slice(jnp.zeros_like(pieces), pieces[g][None], (g, 0, 0))
    for dy, dz in offsets:
        pairs = [(i, ((i // nz + dy) % 2) * nz + (i % nz + dz) % nz) for i in range(ng)]
        dst = lax.rem(yh + dy, 2) * nz + lax.rem(z + dz, nz)
        got = lax.ppermute(pieces[dst], "ga", pairs)
        src = lax.rem(yh + dy, 2) * nz + lax.rem(z - dz + nz, nz)
        stack = lax.dynamic_update_slice(stack, got[None], (src, 0, 0))
    regrouped = stack.transpose(1, 0, 2).reshape(stack.shape[1], -1)
    bt = integrals.T
    full_bt = lax.dynamic_update_slice(jnp.zeros((nb, bk * ng), jnp.float32), bt, (0, g * bk))
    for dy, dz in offsets:
        pairs = [(i, ((i // nz + dy) % 2) * nz + (i % nz + dz) % nz) for i in range(ng)]
        got = lax.ppermute(bt, "ga", pairs)
        src = lax.rem(yh + dy, 2) * nz + lax.rem(z - dz + nz, nz)
        full_bt = lax.dynamic_update_slice(full_bt, got, (0, src * bk))
    full_rows = lax.all_gather(regrouped, "ka", axis=1, tiled=True)
    ladder = lax.dot_general(
        full_rows,
        full_bt,
        (((1,), (1,)), ((), ())),
        precision=lax.Precision.HIGH,
        preferred_element_type=jnp.float32,
    )
    return 0.5 * ladder


def solution(mesh):
    placed = (P(None, ("ka", "ga")), P("ga", "ka"))
    ng = mesh.shape["ga"]
    return jax.shard_map(
        lambda a, b: per_device(ng, a, b), mesh=mesh, in_specs=placed, out_specs=P("ga", "ka"),
        check_vma=False
    )
```

```python
import jax
import jax.numpy as jnp
from jax import lax
from jax.sharding import Mesh
from jax.sharding import PartitionSpec as P


def _offsets(ng):
    nz = ng // 2
    offsets = [(1, dz) for dz in range(nz)] + [(0, dz) for dz in range(nz // 2, 0, -1)]
    return nz, offsets + [(0, dz) for dz in range(nz // 2 + 1, nz)]


def per_device(ng, nxc, amplitudes, integrals):
    g = lax.axis_index("ga")
    ylo = lax.axis_index("ylo")
    bk, nb = integrals.shape
    nz, offsets = _offsets(ng)
    yh, z = g // nz, lax.rem(g, nz)
    regrouped = lax.all_to_all(amplitudes, "ga", split_axis=0, concat_axis=1, tiled=True)
    kw = regrouped.shape[1]
    other = lax.ppermute(regrouped, "ylo", [(0, 1), (1, 0)])
    pair = jnp.zeros((regrouped.shape[0], 2 * kw), jnp.float32)
    pair = lax.dynamic_update_slice(pair, regrouped, (0, ylo * kw))
    pair = lax.dynamic_update_slice(pair, other, (0, (1 - ylo) * kw))
    full_rows = lax.all_gather(pair, "xc", axis=1, tiled=True)

    bt = integrals.T
    full_bt = jnp.zeros((nb, bk * ng), jnp.float32)
    per = bk // kw

    def place(full_bt, blk, src):
        for h in range(per):
            kb = src * per + h
            pos = lax.rem(kb, nxc) * 2 + kb // nxc
            full_bt = lax.dynamic_update_slice(full_bt, blk[:, h * kw:(h + 1) * kw], (0, pos * kw))
        return full_bt

    full_bt = place(full_bt, bt, g)
    for dy, dz in offsets:
        pairs = [(i, ((i // nz + dy) % 2) * nz + (i % nz + dz) % nz) for i in range(ng)]
        got = lax.ppermute(bt, "ga", pairs)
        src = lax.rem(yh + dy, 2) * nz + lax.rem(z - dz + nz, nz)
        full_bt = place(full_bt, got, src)
    ladder = lax.dot_general(
        full_rows,
        full_bt,
        (((1,), (1,)), ((), ())),
        precision=lax.Precision.HIGH,
        preferred_element_type=jnp.float32,
    )
    return 0.5 * ladder


def solution(mesh):
    ng = mesh.shape["ga"]
    nk = mesh.shape["ka"]
    fine = Mesh(mesh.devices.reshape(ng, 2, nk // 2), ("ga", "ylo", "xc"))
    placed = (P(None, ("ylo", "xc", "ga")), P("ga", ("ylo", "xc")))
    return jax.shard_map(
        lambda a, b: per_device(ng, nk // 2, a, b), mesh=fine, in_specs=placed,
        out_specs=P("ga", ("ylo", "xc")), check_vma=False
    )
```

```python
import jax
import jax.numpy as jnp
from jax import lax
from jax.experimental.layout import Layout, with_layout_constraint
from jax.sharding import Mesh
from jax.sharding import PartitionSpec as P


def _offsets(ng):
    nz = ng // 2
    offsets = [(1, dz) for dz in range(nz)] + [(0, dz) for dz in range(nz // 2, 0, -1)]
    return nz, offsets + [(0, dz) for dz in range(nz // 2 + 1, nz)]


def per_device(ng, nxc, amplitudes, integrals):
    g = lax.axis_index("ga")
    ylo = lax.axis_index("ylo")
    bk, nb = integrals.shape
    nz, offsets = _offsets(ng)
    yh, z = g // nz, lax.rem(g, nz)
    regrouped = lax.all_to_all(amplitudes, "ga", split_axis=0, concat_axis=1, tiled=True)
    kw = regrouped.shape[1]
    other = lax.ppermute(regrouped, "ylo", [(0, 1), (1, 0)])
    pair = jnp.zeros((regrouped.shape[0], 2 * kw), jnp.float32)
    pair = lax.dynamic_update_slice(pair, regrouped, (0, ylo * kw))
    pair = lax.dynamic_update_slice(pair, other, (0, (1 - ylo) * kw))
    full_rows = lax.all_gather(pair, "xc", axis=1, tiled=True)

    bt = integrals.T
    full_bt = jnp.zeros((nb, bk * ng), jnp.float32)
    per = bk // kw

    def place(full_bt, blk, src):
        for h in range(per):
            kb = src * per + h
            pos = lax.rem(kb, nxc) * 2 + kb // nxc
            full_bt = lax.dynamic_update_slice(full_bt, blk[:, h * kw:(h + 1) * kw], (0, pos * kw))
        return full_bt

    full_bt = place(full_bt, bt, g)
    for dy, dz in offsets:
        pairs = [(i, ((i // nz + dy) % 2) * nz + (i % nz + dz) % nz) for i in range(ng)]
        got = lax.ppermute(bt, "ga", pairs)
        src = lax.rem(yh + dy, 2) * nz + lax.rem(z - dz + nz, nz)
        full_bt = place(full_bt, got, src)
    ladder_t = lax.dot_general(
        full_bt,
        full_rows,
        (((1,), (1,)), ((), ())),
        precision=lax.Precision.HIGH,
        preferred_element_type=jnp.float32,
    )
    ladder_t = with_layout_constraint(ladder_t, Layout(major_to_minor=(0, 1)))
    return (0.5 * ladder_t).T


def solution(mesh):
    ng = mesh.shape["ga"]
    nk = mesh.shape["ka"]
    fine = Mesh(mesh.devices.reshape(ng, 2, nk // 2), ("ga", "ylo", "xc"))
    placed = (P(None, ("ylo", "xc", "ga")), P("ga", ("ylo", "xc")))
    return jax.shard_map(
        lambda a, b: per_device(ng, nk // 2, a, b), mesh=fine, in_specs=placed,
        out_specs=P("ga", ("ylo", "xc")), check_vma=False
    )
```

```python
import jax
import jax.numpy as jnp
from jax import lax
from jax.experimental.layout import Layout, with_layout_constraint
from jax.sharding import Mesh
from jax.sharding import PartitionSpec as P


def per_device(ng, nxc, amplitudes, integrals):
    g = lax.axis_index("ga")
    ylo = lax.axis_index("ylo")
    bk, nb = integrals.shape
    nz = ng // 2
    yh, z = g // nz, lax.rem(g, nz)
    regrouped = lax.all_to_all(amplitudes, "ga", split_axis=0, concat_axis=1, tiled=True)
    kw = regrouped.shape[1]
    other = lax.ppermute(regrouped, "ylo", [(0, 1), (1, 0)])
    pair = jnp.zeros((regrouped.shape[0], 2 * kw), jnp.float32)
    pair = lax.dynamic_update_slice(pair, regrouped, (0, ylo * kw))
    pair = lax.dynamic_update_slice(pair, other, (0, (1 - ylo) * kw))
    full_rows = lax.all_gather(pair, "xc", axis=1, tiled=True)

    bt = integrals.T
    full_bt = jnp.zeros((nb, bk * ng), jnp.float32)
    per = bk // kw

    def place(full_bt, blk, src):
        for h in range(per):
            kb = src * per + h
            pos = lax.rem(kb, nxc) * 2 + kb // nxc
            full_bt = lax.dynamic_update_slice(full_bt, blk[:, h * kw:(h + 1) * kw], (0, pos * kw))
        return full_bt

    full_bt = place(full_bt, bt, g)
    across = [(i, ((i // nz + 1) % 2) * nz + i % nz) for i in range(ng)]
    got = lax.ppermute(bt, "ga", across)
    full_bt = place(full_bt, got, (1 - yh) * nz + z)
    pair_b = jnp.concatenate([bt, got], axis=1)
    for dz in [nz // 2] + [d for d in range(1, nz) if d != nz // 2]:
        pairs = [(i, (i // nz) * nz + (i % nz + dz) % nz) for i in range(ng)]
        got2 = lax.ppermute(pair_b, "ga", pairs)
        zs = lax.rem(z - dz + nz, nz)
        full_bt = place(full_bt, got2[:, :bk], yh * nz + zs)
        full_bt = place(full_bt, got2[:, bk:], (1 - yh) * nz + zs)
    ladder_t = lax.dot_general(
        full_bt,
        full_rows,
        (((1,), (1,)), ((), ())),
        precision=lax.Precision.HIGH,
        preferred_element_type=jnp.float32,
    )
    ladder_t = with_layout_constraint(ladder_t, Layout(major_to_minor=(0, 1)))
    return (0.5 * ladder_t).T


def solution(mesh):
    ng = mesh.shape["ga"]
    nk = mesh.shape["ka"]
    fine = Mesh(mesh.devices.reshape(ng, 2, nk // 2), ("ga", "ylo", "xc"))
    placed = (P(None, ("ylo", "xc", "ga")), P("ga", ("ylo", "xc")))
    return jax.shard_map(
        lambda a, b: per_device(ng, nk // 2, a, b), mesh=fine, in_specs=placed,
        out_specs=P("ga", ("ylo", "xc")), check_vma=False
    )
```

```python
import jax
import jax.numpy as jnp
from jax import lax
from jax.experimental.layout import Layout, with_layout_constraint
from jax.sharding import Mesh
from jax.sharding import PartitionSpec as P


def _offsets(ng):
    nz = ng // 2
    offsets = [(1, dz) for dz in range(nz)] + [(0, dz) for dz in range(nz // 2, 0, -1)]
    return nz, offsets + [(0, dz) for dz in range(nz // 2 + 1, nz)]


def per_device(ng, nxc, amplitudes, integrals):
    nz = ng // 2
    g = lax.axis_index("yh") * nz + lax.axis_index("zz")
    ylo = lax.axis_index("ylo")
    bk, nb = integrals.shape
    nz, offsets = _offsets(ng)
    yh, z = g // nz, lax.rem(g, nz)
    half = lax.all_to_all(amplitudes, "yh", split_axis=0, concat_axis=1, tiled=True)
    quarter = lax.all_to_all(half, "zz", split_axis=0, concat_axis=1, tiled=True)
    cw = amplitudes.shape[1]
    regrouped = quarter.reshape(-1, nz, 2, cw).transpose(0, 2, 1, 3).reshape(quarter.shape[0], -1)
    kw = regrouped.shape[1]
    other = lax.ppermute(regrouped, "ylo", [(0, 1), (1, 0)])
    pair = jnp.zeros((regrouped.shape[0], 2 * kw), jnp.float32)
    pair = lax.dynamic_update_slice(pair, regrouped, (0, ylo * kw))
    pair = lax.dynamic_update_slice(pair, other, (0, (1 - ylo) * kw))
    full_rows = lax.all_gather(pair, "xc", axis=1, tiled=True)

    bt = integrals.T
    full_bt = jnp.zeros((nb, bk * ng), jnp.float32)
    per = bk // kw

    def place(full_bt, blk, src):
        for h in range(per):
            kb = src * per + h
            pos = lax.rem(kb, nxc) * 2 + kb // nxc
            full_bt = lax.dynamic_update_slice(full_bt, blk[:, h * kw:(h + 1) * kw], (0, pos * kw))
        return full_bt

    full_bt = place(full_bt, bt, g)
    for dy, dz in offsets:
        pairs = [(i, ((i // nz + dy) % 2) * nz + (i % nz + dz) % nz) for i in range(ng)]
        got = lax.ppermute(bt, ("yh", "zz"), pairs)
        src = lax.rem(yh + dy, 2) * nz + lax.rem(z - dz + nz, nz)
        full_bt = place(full_bt, got, src)
    ladder_t = lax.dot_general(
        full_bt,
        full_rows,
        (((1,), (1,)), ((), ())),
        precision=lax.Precision.HIGH,
        preferred_element_type=jnp.float32,
    )
    ladder_t = with_layout_constraint(ladder_t, Layout(major_to_minor=(0, 1)))
    return (0.5 * ladder_t).T


def solution(mesh):
    ng = mesh.shape["ga"]
    nk = mesh.shape["ka"]
    fine = Mesh(mesh.devices.reshape(2, ng // 2, 2, nk // 2), ("yh", "zz", "ylo", "xc"))
    placed = (P(None, ("ylo", "xc", "yh", "zz")), P(("yh", "zz"), ("ylo", "xc")))
    return jax.shard_map(
        lambda a, b: per_device(ng, nk // 2, a, b), mesh=fine, in_specs=placed,
        out_specs=P(("yh", "zz"), ("ylo", "xc")), check_vma=False
    )
```

```python
import jax
import jax.numpy as jnp
from jax import lax
from jax.experimental.layout import Layout, with_layout_constraint
from jax.sharding import Mesh
from jax.sharding import PartitionSpec as P


def _offsets(ng):
    nz = ng // 2
    offsets = [(1, dz) for dz in range(nz)] + [(0, dz) for dz in range(nz // 2, 0, -1)]
    return nz, offsets + [(0, dz) for dz in range(nz // 2 + 1, nz)]


def per_device(ng, nxc, amplitudes, integrals):
    g = lax.axis_index("ga")
    bk, nb = integrals.shape
    nz, offsets = _offsets(ng)
    yh, z = g // nz, lax.rem(g, nz)
    cw = amplitudes.shape[1]
    kw = ng * cw
    twice = jnp.repeat(amplitudes.reshape(ng, -1, cw), 2, axis=0).reshape(-1, cw)
    both = lax.all_to_all(twice, ("ga", "ylo"), split_axis=0, concat_axis=1, tiled=True)
    rows = both.shape[0]
    pair = both.reshape(rows, ng, 2, cw).transpose(0, 2, 1, 3).reshape(rows, 2 * kw)
    full_rows = lax.all_gather(pair, "xc", axis=1, tiled=True)

    bt = integrals.T
    full_bt = jnp.zeros((nb, bk * ng), jnp.float32)
    per = bk // kw

    def place(full_bt, blk, src):
        for h in range(per):
            kb = src * per + h
            pos = lax.rem(kb, nxc) * 2 + kb // nxc
            full_bt = lax.dynamic_update_slice(full_bt, blk[:, h * kw:(h + 1) * kw], (0, pos * kw))
        return full_bt

    full_bt = place(full_bt, bt, g)
    for dy, dz in offsets:
        pairs = [(i, ((i // nz + dy) % 2) * nz + (i % nz + dz) % nz) for i in range(ng)]
        got = lax.ppermute(bt, "ga", pairs)
        src = lax.rem(yh + dy, 2) * nz + lax.rem(z - dz + nz, nz)
        full_bt = place(full_bt, got, src)
    ladder_t = lax.dot_general(
        full_bt,
        full_rows,
        (((1,), (1,)), ((), ())),
        precision=lax.Precision.HIGH,
        preferred_element_type=jnp.float32,
    )
    ladder_t = with_layout_constraint(ladder_t, Layout(major_to_minor=(0, 1)))
    return (0.5 * ladder_t).T


def solution(mesh):
    ng = mesh.shape["ga"]
    nk = mesh.shape["ka"]
    fine = Mesh(mesh.devices.reshape(ng, 2, nk // 2), ("ga", "ylo", "xc"))
    placed = (P(None, ("ylo", "xc", "ga")), P("ga", ("ylo", "xc")))
    return jax.shard_map(
        lambda a, b: per_device(ng, nk // 2, a, b), mesh=fine, in_specs=placed,
        out_specs=P("ga", ("ylo", "xc")), check_vma=False
    )
```

```python
import jax
import jax.numpy as jnp
from jax import lax
from jax.experimental import pallas as pl
from jax.experimental.layout import Layout, with_layout_constraint
from jax.sharding import Mesh
from jax.sharding import PartitionSpec as P


def _offsets(ng):
    nz = ng // 2
    offsets = [(1, dz) for dz in range(nz)] + [(0, dz) for dz in range(nz // 2, 0, -1)]
    return nz, offsets + [(0, dz) for dz in range(nz // 2 + 1, nz)]


def per_device(ng, nxc, amplitudes, integrals):
    g = lax.axis_index("ga")
    bk, nb = integrals.shape
    nz, offsets = _offsets(ng)
    yh, z = g // nz, lax.rem(g, nz)
    cw = amplitudes.shape[1]
    kw = ng * cw
    twice = jnp.repeat(amplitudes.reshape(ng, -1, cw), 2, axis=0).reshape(-1, cw)
    both = lax.all_to_all(twice, ("ga", "ylo"), split_axis=0, concat_axis=1, tiled=True)
    rows = both.shape[0]
    pair = both.reshape(rows, ng, 2, cw).transpose(0, 2, 1, 3).reshape(rows, 2 * kw)
    full_rows = lax.all_gather(pair, "xc", axis=1, tiled=True)

    bt = integrals.T
    full_bt = jnp.zeros((nb, bk * ng), jnp.float32)
    per = bk // kw

    def place(full_bt, blk, src):
        for h in range(per):
            kb = src * per + h
            pos = lax.rem(kb, nxc) * 2 + kb // nxc
            full_bt = lax.dynamic_update_slice(full_bt, blk[:, h * kw:(h + 1) * kw], (0, pos * kw))
        return full_bt

    full_bt = place(full_bt, bt, g)
    for dy, dz in offsets:
        pairs = [(i, ((i // nz + dy) % 2) * nz + (i % nz + dz) % nz) for i in range(ng)]
        got = lax.ppermute(bt, "ga", pairs)
        src = lax.rem(yh + dy, 2) * nz + lax.rem(z - dz + nz, nz)
        full_bt = place(full_bt, got, src)
    ladder_t = lax.dot_general(
        full_bt,
        full_rows,
        (((1,), (1,)), ((), ())),
        precision=lax.Precision.HIGH,
        preferred_element_type=jnp.float32,
    )
    ladder_t = with_layout_constraint(ladder_t, Layout(major_to_minor=(0, 1)))
    return _scaled_transpose(ladder_t)


def _transpose_kernel(x_ref, o_ref):
    o_ref[...] = (0.5 * x_ref[...]).T


def _scaled_transpose(x):
    n, m = x.shape
    tb = 256
    return pl.pallas_call(
        _transpose_kernel,
        out_shape=jax.ShapeDtypeStruct((m, n), x.dtype),
        grid=(pl.cdiv(m, tb),),
        in_specs=[pl.BlockSpec((n, tb), lambda i: (0, i))],
        out_specs=pl.BlockSpec((tb, n), lambda i: (i, 0)),
        cost_estimate=pl.CostEstimate(flops=n * m, bytes_accessed=8 * n * m, transcendentals=0),
    )(x)


def solution(mesh):
    ng = mesh.shape["ga"]
    nk = mesh.shape["ka"]
    fine = Mesh(mesh.devices.reshape(ng, 2, nk // 2), ("ga", "ylo", "xc"))
    placed = (P(None, ("ylo", "xc", "ga")), P("ga", ("ylo", "xc")))
    return jax.shard_map(
        lambda a, b: per_device(ng, nk // 2, a, b), mesh=fine, in_specs=placed,
        out_specs=P("ga", ("ylo", "xc")), check_vma=False
    )
```

```python
import jax
import jax.numpy as jnp
from jax import lax
from jax.experimental.layout import Layout, with_layout_constraint
from jax.sharding import Mesh
from jax.sharding import PartitionSpec as P


def _offsets(ng):
    nz = ng // 2
    offsets = [(1, dz) for dz in range(nz)] + [(0, dz) for dz in range(nz // 2, 0, -1)]
    return nz, offsets + [(0, dz) for dz in range(nz // 2 + 1, nz)]


def per_device(ng, nxc, amplitudes, integrals):
    g = lax.axis_index("ga")
    bk, nb = integrals.shape
    nz, offsets = _offsets(ng)
    yh, z = g // nz, lax.rem(g, nz)
    cw = amplitudes.shape[1]
    kw = ng * cw
    twice = jnp.repeat(amplitudes.reshape(ng, -1, cw), 2, axis=0).reshape(-1, cw)
    both = lax.all_to_all(twice, ("ga", "ylo"), split_axis=0, concat_axis=1, tiled=True)
    rows = both.shape[0]
    pair = both.reshape(rows, ng, 2, cw).transpose(0, 2, 1, 3).reshape(rows, 2 * kw)
    full_rows = lax.all_gather(pair, "xc", axis=1, tiled=True)

    bt = integrals.T
    full_bt = jnp.zeros((nb, bk * ng), jnp.float32)
    per = bk // kw

    def place(full_bt, blk, src):
        for h in range(per):
            kb = src * per + h
            pos = lax.rem(kb, nxc) * 2 + kb // nxc
            full_bt = lax.dynamic_update_slice(full_bt, blk[:, h * kw:(h + 1) * kw], (0, pos * kw))
        return full_bt

    got = lax.all_to_all(jnp.broadcast_to(bt, (ng,) + bt.shape), "ga", 0, 0, tiled=True)
    rows = full_rows.shape[0]
    a_k = full_rows.reshape(rows, nxc, 2, kw).transpose(0, 2, 1, 3).reshape(rows, ng, bk)
    ladder_t = lax.dot_general(
        got,
        a_k,
        (((0, 2), (1, 2)), ((), ())),
        precision=lax.Precision.HIGH,
        preferred_element_type=jnp.float32,
    )
    ladder_t = with_layout_constraint(ladder_t, Layout(major_to_minor=(0, 1)))
    return (0.5 * ladder_t).T


def solution(mesh):
    ng = mesh.shape["ga"]
    nk = mesh.shape["ka"]
    fine = Mesh(mesh.devices.reshape(ng, 2, nk // 2), ("ga", "ylo", "xc"))
    placed = (P(None, ("ylo", "xc", "ga")), P("ga", ("ylo", "xc")))
    return jax.shard_map(
        lambda a, b: per_device(ng, nk // 2, a, b), mesh=fine, in_specs=placed,
        out_specs=P("ga", ("ylo", "xc")), check_vma=False
    )
```

```python
import jax
import jax.numpy as jnp
from jax import lax
from jax.experimental.layout import Layout, with_layout_constraint
from jax.sharding import Mesh
from jax.sharding import PartitionSpec as P


def _offsets(ng):
    nz = ng // 2
    offsets = [(1, dz) for dz in range(nz)] + [(0, dz) for dz in range(nz // 2, 0, -1)]
    return nz, offsets + [(0, dz) for dz in range(nz // 2 + 1, nz)]


def per_device(ng, nxc, amplitudes, integrals):
    g = lax.axis_index("ga")
    bk, nb = integrals.shape
    nz, offsets = _offsets(ng)
    yh, z = g // nz, lax.rem(g, nz)
    cw = amplitudes.shape[1]
    kw = ng * cw
    twice = jnp.repeat(amplitudes.reshape(ng, -1, cw), 2, axis=0).reshape(-1, cw)
    both = lax.all_to_all(twice, ("ga", "ylo"), split_axis=0, concat_axis=1, tiled=True)
    rows = both.shape[0]
    pair = both.reshape(rows, ng, 2, cw).transpose(0, 2, 1, 3).reshape(rows, 2 * kw)
    full_rows = lax.all_gather(pair, "xc", axis=1, tiled=True)

    bt = integrals.T
    full_bt = jnp.zeros((nb, bk * ng), jnp.float32)
    per = bk // kw

    def place(full_bt, blk, src):
        for h in range(per):
            kb = src * per + h
            pos = lax.rem(kb, nxc) * 2 + kb // nxc
            full_bt = lax.dynamic_update_slice(full_bt, blk[:, h * kw:(h + 1) * kw], (0, pos * kw))
        return full_bt

    got = lax.all_to_all(jnp.broadcast_to(bt, (ng,) + bt.shape), "ga", 0, 0, tiled=True)
    hx = nxc // 2
    full_bt = got.reshape(2, hx, nb, per, kw).transpose(2, 1, 3, 0, 4).reshape(nb, ng * bk)
    a_k = full_rows
    ladder_t = lax.dot_general(
        full_bt,
        a_k,
        (((1,), (1,)), ((), ())),
        precision=lax.Precision.HIGH,
        preferred_element_type=jnp.float32,
    )
    ladder_t = with_layout_constraint(ladder_t, Layout(major_to_minor=(0, 1)))
    return (0.5 * ladder_t).T


def solution(mesh):
    ng = mesh.shape["ga"]
    nk = mesh.shape["ka"]
    fine = Mesh(mesh.devices.reshape(ng, 2, nk // 2), ("ga", "ylo", "xc"))
    placed = (P(None, ("ylo", "xc", "ga")), P("ga", ("ylo", "xc")))
    return jax.shard_map(
        lambda a, b: per_device(ng, nk // 2, a, b), mesh=fine, in_specs=placed,
        out_specs=P("ga", ("ylo", "xc")), check_vma=False
    )
```

```python
import jax
import jax.numpy as jnp
from jax import lax
from jax.experimental import pallas as pl
from jax.experimental.layout import Layout, with_layout_constraint
from jax.sharding import Mesh
from jax.sharding import PartitionSpec as P


def _offsets(ng):
    nz = ng // 2
    offsets = [(1, dz) for dz in range(nz)] + [(0, dz) for dz in range(nz // 2, 0, -1)]
    return nz, offsets + [(0, dz) for dz in range(nz // 2 + 1, nz)]


def _copy_kernel(x_ref, o_ref):
    o_ref[...] = x_ref[...]


def per_device(ng, nxc, amplitudes, integrals):
    g = lax.axis_index("ga")
    bk, nb = integrals.shape
    nz, offsets = _offsets(ng)
    yh, z = g // nz, lax.rem(g, nz)
    cw = amplitudes.shape[1]
    kw = ng * cw
    twice = jnp.repeat(amplitudes.reshape(ng, -1, cw), 2, axis=0).reshape(-1, cw)
    both = lax.all_to_all(twice, ("ga", "ylo"), split_axis=0, concat_axis=1, tiled=True)
    rows = both.shape[0]
    pair = both.reshape(rows, ng, 2, cw).transpose(0, 2, 1, 3).reshape(rows, 2 * kw)
    full_rows = lax.all_gather(pair, "xc", axis=1, tiled=True)

    bt = integrals.T
    full_bt = jnp.zeros((nb, bk * ng), jnp.float32)
    per = bk // kw

    def place(full_bt, blk, src):
        for h in range(per):
            kb = src * per + h
            pos = lax.rem(kb, nxc) * 2 + kb // nxc
            full_bt = lax.dynamic_update_slice(full_bt, blk[:, h * kw:(h + 1) * kw], (0, pos * kw))
        return full_bt

    got = lax.all_to_all(jnp.broadcast_to(bt, (ng,) + bt.shape), "ga", 0, 0, tiled=True)
    nblk = ng * per
    full_bt = pl.pallas_call(
        _copy_kernel,
        out_shape=jax.ShapeDtypeStruct((nb, ng * bk), jnp.float32),
        grid=(nblk,),
        in_specs=[pl.BlockSpec((None, nb, kw), lambda i: (i // per, 0, i % per))],
        out_specs=pl.BlockSpec((nb, kw), lambda i: (0, (i % nxc) * 2 + i // nxc)),
        cost_estimate=pl.CostEstimate(flops=0, bytes_accessed=8 * nb * ng * bk, transcendentals=0),
    )(got)
    a_k = full_rows
    ladder_t = lax.dot_general(
        full_bt,
        a_k,
        (((1,), (1,)), ((), ())),
        precision=lax.Precision.HIGH,
        preferred_element_type=jnp.float32,
    )
    ladder_t = with_layout_constraint(ladder_t, Layout(major_to_minor=(0, 1)))
    return (0.5 * ladder_t).T


def solution(mesh):
    ng = mesh.shape["ga"]
    nk = mesh.shape["ka"]
    fine = Mesh(mesh.devices.reshape(ng, 2, nk // 2), ("ga", "ylo", "xc"))
    placed = (P(None, ("ylo", "xc", "ga")), P("ga", ("ylo", "xc")))
    return jax.shard_map(
        lambda a, b: per_device(ng, nk // 2, a, b), mesh=fine, in_specs=placed,
        out_specs=P("ga", ("ylo", "xc")), check_vma=False
    )
```

```python
import functools

import jax
import jax.numpy as jnp
from jax import lax
from jax.experimental import pallas as pl
from jax.experimental.pallas import tpu as pltpu
from jax.experimental.layout import Layout, with_layout_constraint
from jax.sharding import Mesh
from jax.sharding import PartitionSpec as P


def _offsets(ng):
    nz = ng // 2
    offsets = [(1, dz) for dz in range(nz)] + [(0, dz) for dz in range(nz // 2, 0, -1)]
    return nz, offsets + [(0, dz) for dz in range(nz // 2 + 1, nz)]


def _order_kernel(nxc, per, kw, x_ref, o_ref):
    for kb in range(x_ref.shape[0] * per):
        p = (kb % nxc) * 2 + kb // nxc
        o_ref[:, p * kw:(p + 1) * kw] = x_ref[kb // per, :, (kb % per) * kw:(kb % per + 1) * kw]


def per_device(ng, nxc, amplitudes, integrals):
    g = lax.axis_index("ga")
    bk, nb = integrals.shape
    nz, offsets = _offsets(ng)
    yh, z = g // nz, lax.rem(g, nz)
    cw = amplitudes.shape[1]
    kw = ng * cw
    twice = jnp.repeat(amplitudes.reshape(ng, -1, cw), 2, axis=0).reshape(-1, cw)
    both = lax.all_to_all(twice, ("ga", "ylo"), split_axis=0, concat_axis=1, tiled=True)
    rows = both.shape[0]
    pair = both.reshape(rows, ng, 2, cw).transpose(0, 2, 1, 3).reshape(rows, 2 * kw)
    full_rows = lax.all_gather(pair, "xc", axis=1, tiled=True)

    bt = integrals.T
    full_bt = jnp.zeros((nb, bk * ng), jnp.float32)
    per = bk // kw

    def place(full_bt, blk, src):
        for h in range(per):
            kb = src * per + h
            pos = lax.rem(kb, nxc) * 2 + kb // nxc
            full_bt = lax.dynamic_update_slice(full_bt, blk[:, h * kw:(h + 1) * kw], (0, pos * kw))
        return full_bt

    got = lax.all_to_all(jnp.broadcast_to(bt, (ng,) + bt.shape), "ga", 0, 0, tiled=True)
    full_bt = pl.pallas_call(
        functools.partial(_order_kernel, nxc, per, kw),
        out_shape=jax.ShapeDtypeStruct((nb, ng * bk), jnp.float32),
        in_specs=[pl.BlockSpec(memory_space=pltpu.VMEM)],
        out_specs=pl.BlockSpec(memory_space=pltpu.VMEM),
        cost_estimate=pl.CostEstimate(flops=0, bytes_accessed=8 * nb * ng * bk, transcendentals=0),
    )(got)
    a_k = full_rows
    ladder_t = lax.dot_general(
        full_bt,
        a_k,
        (((1,), (1,)), ((), ())),
        precision=lax.Precision.HIGH,
        preferred_element_type=jnp.float32,
    )
    ladder_t = with_layout_constraint(ladder_t, Layout(major_to_minor=(0, 1)))
    return (0.5 * ladder_t).T


def solution(mesh):
    ng = mesh.shape["ga"]
    nk = mesh.shape["ka"]
    fine = Mesh(mesh.devices.reshape(ng, 2, nk // 2), ("ga", "ylo", "xc"))
    placed = (P(None, ("ylo", "xc", "ga")), P("ga", ("ylo", "xc")))
    return jax.shard_map(
        lambda a, b: per_device(ng, nk // 2, a, b), mesh=fine, in_specs=placed,
        out_specs=P("ga", ("ylo", "xc")), check_vma=False
    )
```

```python
import functools

import jax
import jax.numpy as jnp
from jax import lax
from jax.experimental import pallas as pl
from jax.experimental.pallas import tpu as pltpu
from jax.experimental.layout import Layout, with_layout_constraint
from jax.sharding import Mesh
from jax.sharding import PartitionSpec as P


def _offsets(ng):
    nz = ng // 2
    offsets = [(1, dz) for dz in range(nz)] + [(0, dz) for dz in range(nz // 2, 0, -1)]
    return nz, offsets + [(0, dz) for dz in range(nz // 2 + 1, nz)]


def _order_kernel(nxc, per, kw, x_ref, o_ref):
    for kb in range(x_ref.shape[0] * per):
        p = (kb % nxc) * 2 + kb // nxc
        o_ref[:, p * kw:(p + 1) * kw] = x_ref[kb // per, :, (kb % per) * kw:(kb % per + 1) * kw]


def per_device(ng, nxc, amplitudes, integrals):
    g = lax.axis_index("ga")
    bk, nb = integrals.shape
    nz, offsets = _offsets(ng)
    yh, z = g // nz, lax.rem(g, nz)
    cw = amplitudes.shape[1]
    kw = ng * cw
    twice = jnp.repeat(amplitudes.reshape(ng, -1, cw), 2, axis=0).reshape(-1, cw)
    both = lax.all_to_all(twice, ("ga", "ylo"), split_axis=0, concat_axis=1, tiled=True)
    rows = both.shape[0]
    pair = both.reshape(rows, ng, 2, cw).transpose(0, 2, 1, 3).reshape(rows, 2 * kw)
    full_rows = lax.all_gather(pair.reshape(rows, 2, kw), "xc", axis=2, tiled=True)
    full_rows = full_rows.reshape(rows, -1)

    bt = integrals.T
    full_bt = jnp.zeros((nb, bk * ng), jnp.float32)
    per = bk // kw

    def place(full_bt, blk, src):
        for h in range(per):
            kb = src * per + h
            pos = lax.rem(kb, nxc) * 2 + kb // nxc
            full_bt = lax.dynamic_update_slice(full_bt, blk[:, h * kw:(h + 1) * kw], (0, pos * kw))
        return full_bt

    got = lax.all_to_all(jnp.broadcast_to(bt, (ng,) + bt.shape), "ga", 0, 0, tiled=True)
    ladder_t = lax.dot_general(
        got,
        full_rows.reshape(rows, ng, bk),
        (((0, 2), (1, 2)), ((), ())),
        precision=lax.Precision.HIGH,
        preferred_element_type=jnp.float32,
    )
    ladder_t = with_layout_constraint(ladder_t, Layout(major_to_minor=(0, 1)))
    return (0.5 * ladder_t).T


def solution(mesh):
    ng = mesh.shape["ga"]
    nk = mesh.shape["ka"]
    fine = Mesh(mesh.devices.reshape(ng, 2, nk // 2), ("ga", "ylo", "xc"))
    placed = (P(None, ("ylo", "xc", "ga")), P("ga", ("ylo", "xc")))
    return jax.shard_map(
        lambda a, b: per_device(ng, nk // 2, a, b), mesh=fine, in_specs=placed,
        out_specs=P("ga", ("ylo", "xc")), check_vma=False
    )
```

```python
import functools

import jax
import jax.numpy as jnp
from jax import lax
from jax.experimental import pallas as pl
from jax.experimental.pallas import tpu as pltpu
from jax.experimental.layout import Layout, with_layout_constraint
from jax.sharding import Mesh
from jax.sharding import PartitionSpec as P


def _offsets(ng):
    nz = ng // 2
    offsets = [(1, dz) for dz in range(nz)] + [(0, dz) for dz in range(nz // 2, 0, -1)]
    return nz, offsets + [(0, dz) for dz in range(nz // 2 + 1, nz)]


def _order_kernel(nxc, per, kw, x_ref, o_ref):
    for kb in range(x_ref.shape[0] * per):
        p = (kb % nxc) * 2 + kb // nxc
        o_ref[:, p * kw:(p + 1) * kw] = x_ref[kb // per, :, (kb % per) * kw:(kb % per + 1) * kw]


def per_device(ng, nxc, amplitudes, integrals):
    g = lax.axis_index("ga")
    bk, nb = integrals.shape
    nz, offsets = _offsets(ng)
    yh, z = g // nz, lax.rem(g, nz)
    cw = amplitudes.shape[1]
    kw = ng * cw
    twice = jnp.repeat(amplitudes.reshape(ng, -1, cw), 2, axis=0).reshape(-1, cw)
    both = lax.all_to_all(twice, ("ga", "ylo"), split_axis=0, concat_axis=1, tiled=True)
    rows = both.shape[0]
    pair = both.reshape(rows, ng, 2, cw).transpose(0, 2, 1, 3).reshape(rows, 2 * kw)
    full_rows = lax.all_gather(pair.reshape(rows, 2, kw), "xc", axis=2, tiled=True)
    full_rows = full_rows.reshape(rows, -1)

    bt = integrals.T
    full_bt = jnp.zeros((nb, bk * ng), jnp.float32)
    per = bk // kw

    def place(full_bt, blk, src):
        for h in range(per):
            kb = src * per + h
            pos = lax.rem(kb, nxc) * 2 + kb // nxc
            full_bt = lax.dynamic_update_slice(full_bt, blk[:, h * kw:(h + 1) * kw], (0, pos * kw))
        return full_bt

    got = lax.all_to_all(jnp.broadcast_to(bt, (ng,) + bt.shape), "ga", 0, 0, tiled=True)
    ladder = lax.dot_general(
        full_rows.reshape(rows, ng, bk),
        got,
        (((1, 2), (0, 2)), ((), ())),
        precision=lax.Precision.HIGH,
        preferred_element_type=jnp.float32,
    )
    return 0.5 * ladder


def solution(mesh):
    ng = mesh.shape["ga"]
    nk = mesh.shape["ka"]
    fine = Mesh(mesh.devices.reshape(ng, 2, nk // 2), ("ga", "ylo", "xc"))
    placed = (P(None, ("ylo", "xc", "ga")), P("ga", ("ylo", "xc")))
    return jax.shard_map(
        lambda a, b: per_device(ng, nk // 2, a, b), mesh=fine, in_specs=placed,
        out_specs=P("ga", ("ylo", "xc")), check_vma=False
    )
```

```python
import functools

import jax
import jax.numpy as jnp
from jax import lax
from jax.experimental import pallas as pl
from jax.experimental.pallas import tpu as pltpu
from jax.experimental.layout import Layout, with_layout_constraint
from jax.sharding import Mesh
from jax.sharding import PartitionSpec as P


def _offsets(ng):
    nz = ng // 2
    offsets = [(1, dz) for dz in range(nz)] + [(0, dz) for dz in range(nz // 2, 0, -1)]
    return nz, offsets + [(0, dz) for dz in range(nz // 2 + 1, nz)]


def _order_kernel(nxc, per, kw, x_ref, o_ref):
    for kb in range(x_ref.shape[0] * per):
        p = (kb % nxc) * 2 + kb // nxc
        o_ref[:, p * kw:(p + 1) * kw] = x_ref[kb // per, :, (kb % per) * kw:(kb % per + 1) * kw]


def per_device(ng, nxc, amplitudes, integrals):
    g = lax.axis_index("ga")
    bk, nb = integrals.shape
    nz, offsets = _offsets(ng)
    yh, z = g // nz, lax.rem(g, nz)
    cw = amplitudes.shape[1]
    kw = ng * cw
    twice = jnp.repeat(amplitudes.reshape(ng, -1, cw), 2, axis=0).reshape(-1, cw)
    both = lax.all_to_all(twice, ("ga", "ylo"), split_axis=0, concat_axis=1, tiled=True)
    rows = both.shape[0]
    pair = both.reshape(rows, ng, 2, cw).transpose(0, 2, 1, 3).reshape(rows, 2 * kw)
    full_rows = lax.all_gather(pair.reshape(rows, 2, kw), "xc", axis=2, tiled=True)
    full_rows = full_rows.reshape(rows, -1)

    bt = integrals.T
    full_bt = jnp.zeros((nb, bk * ng), jnp.float32)
    per = bk // kw

    def place(full_bt, blk, src):
        for h in range(per):
            kb = src * per + h
            pos = lax.rem(kb, nxc) * 2 + kb // nxc
            full_bt = lax.dynamic_update_slice(full_bt, blk[:, h * kw:(h + 1) * kw], (0, pos * kw))
        return full_bt

    got = lax.all_to_all(jnp.broadcast_to(integrals, (ng,) + integrals.shape), "ga", 0, 0, tiled=True)
    ladder_t = lax.dot_general(
        got,
        full_rows.reshape(rows, ng, bk),
        (((0, 1), (1, 2)), ((), ())),
        precision=lax.Precision.HIGH,
        preferred_element_type=jnp.float32,
    )
    ladder_t = with_layout_constraint(ladder_t, Layout(major_to_minor=(0, 1)))
    return (0.5 * ladder_t).T


def solution(mesh):
    ng = mesh.shape["ga"]
    nk = mesh.shape["ka"]
    fine = Mesh(mesh.devices.reshape(ng, 2, nk // 2), ("ga", "ylo", "xc"))
    placed = (P(None, ("ylo", "xc", "ga")), P("ga", ("ylo", "xc")))
    return jax.shard_map(
        lambda a, b: per_device(ng, nk // 2, a, b), mesh=fine, in_specs=placed,
        out_specs=P("ga", ("ylo", "xc")), check_vma=False
    )
```
